32 devices in a mesh: rows: 4 (over z), coarse: 4 (over x, core), fine: 2 (over y).
Axes of the slice: x: 2, y: 2, z: 4, core: 2. Of those that a mesh axis runs over, the one named last changes fastest.
Arguments:
- eigvecs: bfloat16 [2048, 4096], P('rows', ('coarse', 'fine')), may hold values from -6 to 6
- perm: int32 [4096], P(('coarse', 'fine')), may hold values from 0 to 511, as said below
- counts: int32 [8], replicated, may hold values from 1 to 256, as said below
- poles: float32 [4096], replicated, may hold values from 0 to 4096, as said below
- weights: float32 [4096], replicated, may hold values from -10 to 10, as said below
- roots: float32 [4096], P(('coarse', 'fine')), may hold values from 0 to 4096, as said below
Outputs:
- merged: bfloat16 [2048, 4096], P('rows', ('coarse', 'fine'))
The draws below stay inside these ranges and needn't reach their ends.
Inputs may be any that keep to these rules, and one draw needn't show every extreme that they name: `perm`: each aligned block of 512 entries is a permutation of 0 to 511. `counts`: at least one device has exactly 256. Every entry of poles lies 0.2 or more away from every entry of roots. `weights`: magnitudes 0.1 or more. `roots`: every entry lies 0.2 or more away from every entry of poles.
All inputs are finite; a program needn't handle non-finite values.
Results may differ from the reference program's by a relative error of at most 0.0027.
Values may be sent and summed in bfloat16 or wider, within the bound.
A program may use at most 64 MiB of HBM per device.

```python
import jax
import jax.numpy as jnp
from jax import lax

COLS_DEV = 512
UNDEF_MOST = 256
DEVCOLS = 8
NODE = 4096
ROWS = 2048


def draw_perm(key, part):
    keys = jax.random.split(jax.random.fold_in(key, 5), DEVCOLS)
    blocks = jax.vmap(lambda single: jax.random.permutation(single, COLS_DEV))(keys)
    return blocks.reshape(-1).astype(jnp.int32)


def draw_counts(key, part):
    low = max(1, UNDEF_MOST // 8)
    values = jax.random.randint(jax.random.fold_in(key, 7), (DEVCOLS,), low, UNDEF_MOST + 1)
    chosen = jax.random.randint(jax.random.fold_in(key, 9), (), 0, DEVCOLS)
    return values.at[chosen].set(UNDEF_MOST).astype(jnp.int32)


def draw_poles(key, part):
    grid = jax.random.permutation(jax.random.fold_in(key, 11), NODE).astype(jnp.float32)
    jitter = jax.random.uniform(jax.random.fold_in(key, 13), (NODE,), jnp.float32, 0.0, 0.3)
    return grid + jitter


def draw_roots(key, part):
    grid = jax.random.permutation(jax.random.fold_in(key, 23), NODE).astype(jnp.float32)
    jitter = jax.random.uniform(jax.random.fold_in(key, 29), (NODE,), jnp.float32, 0.5, 0.8)
    return grid + jitter


def draw_weights(key, part):
    signs = jnp.where(jax.random.bernoulli(jax.random.fold_in(key, 31), 0.5, (NODE,)), 1.0, -1.0)
    logs = jax.random.uniform(jax.random.fold_in(key, 37), (NODE,), jnp.float32, jnp.log(0.3), jnp.log(3.0))
    return (signs * jnp.exp(logs)).astype(jnp.float32)


def levels(rng, extent, cuts, low, largest):
    def one(axis_at, blocks):
        draws = jax.random.uniform(jax.random.fold_in(jax.random.fold_in(rng, 6), axis_at), (blocks,), jnp.float32, low / len(cuts), largest / len(cuts))
        return jnp.repeat(jnp.exp(draws), extent[axis_at] // blocks).reshape((-1,) + (1,) * (len(extent) - axis_at - 1))

    level = one(*cuts[0])
    for cut in cuts[1:]:
        level = level * one(*cut)
    return level


def gaussian(key, dims, width, bound, cuts=(), kind=jnp.bfloat16):
    drawn = jax.random.normal(key, dims, jnp.float32) * width
    if len(cuts) > 0:
        drawn = levels(key, dims, cuts, -0.22, 0.18) * drawn
    return jnp.clip(drawn, min=-bound, max=bound).astype(kind)


def setup_inputs(seed: int = 0) -> dict:
    seeds = jax.random.split(jax.random.key(seed), 7)
    return {
        "eigvecs": gaussian(seeds[0], (ROWS, NODE), 1.0, 6.0, ((0, 4), (1, 8))),
        "perm": draw_perm(jax.random.fold_in(seeds[6], 71), 0),
        "counts": draw_counts(jax.random.fold_in(seeds[6], 71), 0),
        "poles": draw_poles(jax.random.fold_in(seeds[6], 71), 0),
        "weights": draw_weights(jax.random.fold_in(seeds[6], 71), 0),
        "roots": draw_roots(jax.random.fold_in(seeds[6], 71), 0),
    }


def reference(eigvecs, perm, counts, poles, weights, roots):
    order_total = eigvecs.shape[1]
    device_count = counts.shape[0]
    columns_dev = order_total // device_count
    positions = jnp.arange(order_total, dtype=jnp.int32)
    owners = positions // columns_dev
    gathered_ids = (owners * columns_dev + perm).astype(jnp.int32)
    permuted = jnp.take(eigvecs, gathered_ids, axis=1)
    within = positions % columns_dev
    factor = jnp.where(within < counts[owners], weights, jnp.zeros_like(weights))

    def column_block(device):
        offset = (device * columns_dev).astype(jnp.int32)
        own_roots = lax.dynamic_slice_in_dim(roots, offset, UNDEF_MOST)
        cauchy = factor[:, None] / (poles[:, None] - own_roots[None, :])
        norm = jnp.sqrt(lax.optimization_barrier(jnp.sum(cauchy * cauchy, axis=0)))
        summed = jnp.dot(permuted, cauchy.astype(jnp.bfloat16), preferred_element_type=jnp.float32)
        updated = summed / norm[None, :]
        leading = lax.dynamic_slice_in_dim(permuted, offset, UNDEF_MOST, 1)
        retain = jnp.arange(UNDEF_MOST, dtype=jnp.int32) < counts[device]
        return jnp.where(retain[None, :], updated, leading.astype(jnp.float32)).astype(jnp.bfloat16)
    heads = lax.map(column_block, jnp.arange(device_count, dtype=jnp.int32))
    row_count = eigvecs.shape[0]
    rest = permuted.reshape(row_count, device_count, columns_dev)[:, :, UNDEF_MOST:]
    joined = jnp.concatenate([jnp.transpose(heads, (1, 0, 2)), rest], axis=2)
    return joined.reshape(row_count, order_total)
```

```python
import functools

import jax
import jax.numpy as jnp
from jax import lax
from jax.experimental import pallas as pl
from jax.experimental.pallas import tpu as pltpu
from jax.sharding import PartitionSpec as P

UNDEF_MOST = 256
LANES = 128
CORES = 2
MESH = pl.DeviceIdType.MESH


def repeat(total, body):
    if total <= 8:
        for i in range(total):
            body(i)
    else:
        lax.fori_loop(0, total, lambda i, c: (body(i), c)[1], 0)


def merge_kernel(
    n_coarse, n_fine, pieces, eig_hbm, perm_hbm, counts_hbm, poles_hbm, weights_hbm, roots_hbm, out_hbm,
    eig, perm, counts, poles, weights, roots, select, panel, cauchy, total, rest, lead,
    in_sem, small_sem, out_sem, rest_sem, recv_sem, own_sem, partner_sem, cross_sem,
):
    rows, columns = eig.shape
    live = UNDEF_MOST
    device_total = n_coarse * n_fine
    n_x = n_coarse // CORES
    size = rows // pieces
    coarse = lax.axis_index("coarse")
    fine = lax.axis_index("fine")
    x = coarse // CORES
    core = lax.rem(coarse, CORES)
    other_core = 1 - core

    def owner_of(px, pc, pf):
        return (px * CORES + pc) * n_fine + pf

    def device_of(px, pc, pf):
        return {"coarse": px * CORES + pc, "fine": pf}

    me = owner_of(x, core, fine)
    x_of = lambda i: lax.rem(x + 1 + i, n_x)
    f_of = lambda j: lax.rem(fine + 1 + j, n_fine)
    partner = device_of(x, other_core, fine)

    barrier = pltpu.get_barrier_semaphore()
    pl.semaphore_signal(barrier, inc=1, device_id=partner, device_id_type=MESH)
    for i in range(n_x - 1):
        pl.semaphore_signal(barrier, inc=1, device_id=device_of(x_of(i), core, fine), device_id_type=MESH)
    for j in range(n_fine - 1):
        pl.semaphore_signal(barrier, inc=1, device_id=device_of(x, core, f_of(j)), device_id_type=MESH)

    perm_in = pltpu.make_async_copy(perm_hbm, perm, small_sem.at[0])
    perm_in.start()
    eig_in = []
    for k in range(pieces):
        part = pl.ds(k * size, size)
        copy = pltpu.make_async_copy(eig_hbm.at[part], eig.at[part], in_sem.at[k])
        copy.start()
        eig_in.append(copy)
    small_in = [
        pltpu.make_async_copy(counts_hbm, counts, small_sem.at[1]),
        pltpu.make_async_copy(poles_hbm, poles, small_sem.at[2]),
        pltpu.make_async_copy(weights_hbm, weights, small_sem.at[3]),
        pltpu.make_async_copy(roots_hbm, roots, small_sem.at[4]),
    ]
    for copy in small_in:
        copy.start()

    def send(owner, k, sem, target):
        part = panel.at[owner, pl.ds(k * size, size)]
        return pltpu.make_async_remote_copy(
            src_ref=part, dst_ref=part, send_sem=sem, recv_sem=recv_sem.at[owner, k],
            device_id=target, device_id_type=MESH,
        )

    def arrived(owner, k):
        send(owner, k, partner_sem.at[owner, k], partner).wait_recv()

    def to_partner(owner, k):
        send(owner, k, partner_sem.at[owner, k], partner).start()

    def own_sends(k):
        copies = []
        for j in range(n_fine - 1):
            copies.append(send(me, k, own_sem.at[n_x - 1 + j, k], device_of(x, core, f_of(j))))
        for i in range(n_x - 1):
            copies.append(send(me, k, own_sem.at[i, k], device_of(x_of(i), core, fine)))
        copies.append(send(me, k, partner_sem.at[me, k], partner))
        return copies

    def cross_send(i, j, k):
        first = core == 0
        owner = jnp.where(first, owner_of(x, core, f_of(j)), owner_of(x_of(i), core, fine))
        target = {
            "coarse": jnp.where(first, x_of(i), x) * CORES + core,
            "fine": jnp.where(first, fine, f_of(j)),
        }
        return send(owner, k, cross_sem.at[i * (n_fine - 1) + j, k], target)

    perm_in.wait()
    source = lax.broadcasted_iota(jnp.int32, (columns, LANES), 0)
    for q in range(columns // LANES):
        hit = source == perm[q : q + 1, :]
        select[:, q * LANES : (q + 1) * LANES] = jnp.where(hit, 1.0, 0.0).astype(jnp.bfloat16)

    for k in range(pieces):
        part = pl.ds(k * size, size)
        eig_in[k].wait()
        panel[me, part] = jnp.dot(
            eig[part], select[:, :live], preferred_element_type=jnp.float32
        ).astype(jnp.bfloat16)
        if k == 0:
            pl.semaphore_wait(barrier, n_x + n_fine - 1)
        else:
            for copy in own_sends(k - 1):
                copy.start()
    for copy in small_in:
        copy.wait()
    for copy in own_sends(pieces - 1):
        copy.start()

    width = columns // LANES
    group = 8 // width
    root_row = jnp.concatenate([roots[s : s + 1, :] for s in range(live // LANES)], axis=1)
    within = lax.broadcasted_iota(jnp.int32, (LANES, 1), 0)

    def cauchy_group(t, squares):
        lines = pl.ds(pl.multiple_of(t * 8, 8), 8)
        pole_t = jnp.transpose(poles[lines, :])
        weight_t = jnp.transpose(weights[lines, :])
        for h in range(group):
            block = t * group + h
            count = counts[block]
            for s in range(live // LANES):
                at = h * width + s
                alive = within + s * LANES < count
                factor = jnp.where(alive, weight_t[:, at : at + 1], 0.0)
                value = factor / (pole_t[:, at : at + 1] - root_row)
                squares = squares + jnp.sum(value * value, axis=0, keepdims=True)
                start = pl.multiple_of(block * live + s * LANES, LANES)
                cauchy[pl.ds(start, LANES), :] = value.astype(jnp.bfloat16)
        return squares

    squares = jnp.zeros((1, live), jnp.float32)
    if device_total <= 8:
        for t in range(device_total // group):
            squares = cauchy_group(t, squares)
    else:
        squares = lax.fori_loop(0, device_total // group, cauchy_group, squares)
    scale = 1.0 / jnp.sqrt(squares)

    def product(owner, k):
        start = pl.multiple_of(owner * live, live)
        return jnp.dot(
            panel[owner, pl.ds(k * size, size)], cauchy[pl.ds(start, live), :],
            preferred_element_type=jnp.float32,
        )

    def near(pc):
        return (
            [owner_of(x, pc, fine)]
            + [owner_of(x_of(i), pc, fine) for i in range(n_x - 1)]
            + [owner_of(x, pc, f_of(j)) for j in range(n_fine - 1)]
        )

    crossings = (n_x - 1) * (n_fine - 1)

    def spread(total_steps, body):
        repeat(total_steps, lambda n: body(n // (n_fine - 1), n % (n_fine - 1)))

    def add(owners, k, fresh=False):
        part = pl.ds(k * size, size)
        value = None if fresh else total[part]
        for owner in owners:
            term = product(owner, k)
            value = term if value is None else value + term
        total[part] = value

    def add_near_other(k):
        for owner in near(other_core):
            arrived(owner, k)
        add(near(other_core), k)

    rest_out = pltpu.make_async_copy(rest, out_hbm.at[:, pl.ds(live, columns - live)], rest_sem)

    for k in range(pieces):
        for owner in near(core)[1:]:
            arrived(owner, k)
            to_partner(owner, k)
        spread(crossings, lambda i, j: cross_send(i, j, k).start())
        if k == 0:
            for r in range(pieces):
                part = pl.ds(r * size, size)
                rest[part] = jnp.dot(
                    eig[part], select[:, live:], preferred_element_type=jnp.float32
                ).astype(jnp.bfloat16)
            rest_out.start()
        add(near(core), k, fresh=True)
        if k >= 1:
            add_near_other(k - 1)

    retain = lax.broadcasted_iota(jnp.int32, (1, live), 1) < counts[me]

    def lead_copy(k):
        part = pl.ds(k * size, size)
        return pltpu.make_async_copy(lead.at[part], out_hbm.at[part, pl.ds(0, live)], out_sem.at[k])

    def finish(k):
        part = pl.ds(k * size, size)

        def last(i, j):
            owner = owner_of(x_of(i), other_core, f_of(j))
            arrived(owner, k)
            add([owner], k)

        spread(crossings, last)
        updated = total[part] * scale
        kept = panel[me, part].astype(jnp.float32)
        lead[part] = jnp.where(retain, updated, kept).astype(jnp.bfloat16)
        lead_copy(k).start()

    for k in range(pieces):
        def relay(i, j):
            owner = owner_of(x_of(i), core, f_of(j))
            arrived(owner, k)
            to_partner(owner, k)

        spread(crossings, relay)
        if k == 0:
            add_near_other(pieces - 1)
        spread(crossings, lambda i, j: add([owner_of(x_of(i), core, f_of(j))], k))
        if k >= 1:
            finish(k - 1)
    finish(pieces - 1)

    for k in range(pieces):
        for copy in own_sends(k):
            copy.wait_send()
        for owner in near(core)[1:]:
            send(owner, k, partner_sem.at[owner, k], partner).wait_send()

        def drain(i, j):
            cross_send(i, j, k).wait_send()
            owner = owner_of(x_of(i), core, f_of(j))
            send(owner, k, partner_sem.at[owner, k], partner).wait_send()

        spread(crossings, drain)
    rest_out.wait()
    for k in range(pieces):
        lead_copy(k).wait()


def per_device(n_coarse, n_fine, eigvecs, perm, counts, poles, weights, roots):
    rows, columns = eigvecs.shape
    live = UNDEF_MOST
    device_total = n_coarse * n_fine
    pieces = 4 if device_total <= 8 else 2
    hops = n_coarse // CORES - 1 + n_fine - 1
    crossings = max(1, (n_coarse // CORES - 1) * (n_fine - 1))
    lanes = lambda v: v.reshape(-1, LANES)
    anywhere = pl.BlockSpec(memory_space=pl.ANY)
    return pl.pallas_call(
        functools.partial(merge_kernel, n_coarse, n_fine, pieces),
        out_shape=jax.ShapeDtypeStruct((rows, columns), jnp.bfloat16),
        in_specs=[anywhere] * 6,
        out_specs=anywhere,
        scratch_shapes=[
            pltpu.VMEM((rows, columns), jnp.bfloat16),
            pltpu.VMEM((columns // LANES, LANES), jnp.int32),
            pltpu.SMEM((device_total,), jnp.int32),
            pltpu.VMEM((device_total * columns // LANES, LANES), jnp.float32),
            pltpu.VMEM((device_total * columns // LANES, LANES), jnp.float32),
            pltpu.VMEM((columns // LANES, LANES), jnp.float32),
            pltpu.VMEM((columns, columns), jnp.bfloat16),
            pltpu.VMEM((device_total, rows, live), jnp.bfloat16),
            pltpu.VMEM((device_total * live, live), jnp.bfloat16),
            pltpu.VMEM((rows, live), jnp.float32),
            pltpu.VMEM((rows, columns - live), jnp.bfloat16),
            pltpu.VMEM((rows, live), jnp.bfloat16),
            pltpu.SemaphoreType.DMA((pieces,)),
            pltpu.SemaphoreType.DMA((5,)),
            pltpu.SemaphoreType.DMA((pieces,)),
            pltpu.SemaphoreType.DMA,
            pltpu.SemaphoreType.DMA((device_total, pieces)),
            pltpu.SemaphoreType.DMA((hops, pieces)),
            pltpu.SemaphoreType.DMA((device_total, pieces)),
            pltpu.SemaphoreType.DMA((crossings, pieces)),
        ],
        compiler_params=pltpu.CompilerParams(
            collective_id=0, has_side_effects=True, vmem_limit_bytes=48 * 2**20
        ),
        name="merge",
    )(eigvecs, lanes(perm), counts, lanes(poles), lanes(weights), lanes(roots))


def solution(mesh):
    in_specs = (
        P("rows", ("coarse", "fine")),
        P(("coarse", "fine")),
        P(),
        P(),
        P(),
        P(("coarse", "fine")),
    )
    out_specs = P("rows", ("coarse", "fine"))
    body = functools.partial(per_device, mesh.shape["coarse"], mesh.shape["fine"])
    return jax.shard_map(
        body, mesh=mesh, in_specs=in_specs, out_specs=out_specs, check_vma=False
    )
```

```python
import functools

import jax
import jax.numpy as jnp
from jax import lax
from jax.experimental import pallas as pl
from jax.experimental.pallas import tpu as pltpu
from jax.sharding import PartitionSpec as P

UNDEF_MOST = 256
LANES = 128
CORES = 2
MESH = pl.DeviceIdType.MESH


def repeat(total, body):
    if total <= 8:
        for i in range(total):
            body(i)
    else:
        lax.fori_loop(0, total, lambda i, c: (body(i), c)[1], 0)


def merge_kernel(
    n_coarse, n_fine, pieces, eig_hbm, perm_hbm, counts_hbm, poles_hbm, weights_hbm, roots_hbm, out,
    eig, perm, counts, poles, weights, roots, select, panel, cauchy, total,
    in_sem, small_sem, recv_sem, own_sem, partner_sem, cross_sem,
):
    rows, columns = eig.shape
    live = UNDEF_MOST
    device_total = n_coarse * n_fine
    n_x = n_coarse // CORES
    size = rows // pieces
    coarse = lax.axis_index("coarse")
    fine = lax.axis_index("fine")
    x = coarse // CORES
    core = lax.rem(coarse, CORES)
    other_core = 1 - core

    def owner_of(px, pc, pf):
        return (px * CORES + pc) * n_fine + pf

    def device_of(px, pc, pf):
        return {"coarse": px * CORES + pc, "fine": pf}

    me = owner_of(x, core, fine)
    x_of = lambda i: lax.rem(x + 1 + i, n_x)
    f_of = lambda j: lax.rem(fine + 1 + j, n_fine)
    partner = device_of(x, other_core, fine)

    barrier = pltpu.get_barrier_semaphore()
    pl.semaphore_signal(barrier, inc=1, device_id=partner, device_id_type=MESH)
    for i in range(n_x - 1):
        pl.semaphore_signal(barrier, inc=1, device_id=device_of(x_of(i), core, fine), device_id_type=MESH)
    for j in range(n_fine - 1):
        pl.semaphore_signal(barrier, inc=1, device_id=device_of(x, core, f_of(j)), device_id_type=MESH)

    perm_in = pltpu.make_async_copy(perm_hbm, perm, small_sem.at[0])
    perm_in.start()
    eig_in = []
    for k in range(pieces):
        part = pl.ds(k * size, size)
        copy = pltpu.make_async_copy(eig_hbm.at[part], eig.at[part], in_sem.at[k])
        copy.start()
        eig_in.append(copy)
    small_in = [
        pltpu.make_async_copy(counts_hbm, counts, small_sem.at[1]),
        pltpu.make_async_copy(poles_hbm, poles, small_sem.at[2]),
        pltpu.make_async_copy(weights_hbm, weights, small_sem.at[3]),
        pltpu.make_async_copy(roots_hbm, roots, small_sem.at[4]),
    ]
    for copy in small_in:
        copy.start()

    def send(owner, k, sem, target):
        part = panel.at[owner, pl.ds(k * size, size)]
        return pltpu.make_async_remote_copy(
            src_ref=part, dst_ref=part, send_sem=sem, recv_sem=recv_sem.at[owner, k],
            device_id=target, device_id_type=MESH,
        )

    def arrived(owner, k):
        send(owner, k, partner_sem.at[owner, k], partner).wait_recv()

    def to_partner(owner, k):
        send(owner, k, partner_sem.at[owner, k], partner).start()

    def own_sends(k):
        copies = []
        for j in range(n_fine - 1):
            copies.append(send(me, k, own_sem.at[n_x - 1 + j, k], device_of(x, core, f_of(j))))
        for i in range(n_x - 1):
            copies.append(send(me, k, own_sem.at[i, k], device_of(x_of(i), core, fine)))
        copies.append(send(me, k, partner_sem.at[me, k], partner))
        return copies

    def cross_send(i, j, k):
        first = core == 0
        owner = jnp.where(first, owner_of(x, core, f_of(j)), owner_of(x_of(i), core, fine))
        target = {
            "coarse": jnp.where(first, x_of(i), x) * CORES + core,
            "fine": jnp.where(first, fine, f_of(j)),
        }
        return send(owner, k, cross_sem.at[i * (n_fine - 1) + j, k], target)

    perm_in.wait()
    source = lax.broadcasted_iota(jnp.int32, (columns, LANES), 0)
    for q in range(columns // LANES):
        hit = source == perm[q : q + 1, :]
        select[:, q * LANES : (q + 1) * LANES] = jnp.where(hit, 1.0, 0.0).astype(jnp.bfloat16)

    for k in range(pieces):
        part = pl.ds(k * size, size)
        eig_in[k].wait()
        panel[me, part] = jnp.dot(
            eig[part], select[:, :live], preferred_element_type=jnp.float32
        ).astype(jnp.bfloat16)
        if k == 0:
            pl.semaphore_wait(barrier, n_x + n_fine - 1)
        else:
            for copy in own_sends(k - 1):
                copy.start()
    for copy in small_in:
        copy.wait()
    for copy in own_sends(pieces - 1):
        copy.start()

    width = columns // LANES
    group = 8 // width
    root_row = jnp.concatenate([roots[s : s + 1, :] for s in range(live // LANES)], axis=1)
    within = lax.broadcasted_iota(jnp.int32, (LANES, 1), 0)

    def cauchy_group(t, squares):
        lines = pl.ds(pl.multiple_of(t * 8, 8), 8)
        pole_t = jnp.transpose(poles[lines, :])
        weight_t = jnp.transpose(weights[lines, :])
        for h in range(group):
            block = t * group + h
            count = counts[block]
            for s in range(live // LANES):
                at = h * width + s
                alive = within + s * LANES < count
                factor = jnp.where(alive, weight_t[:, at : at + 1], 0.0)
                value = factor / (pole_t[:, at : at + 1] - root_row)
                squares = squares + jnp.sum(value * value, axis=0, keepdims=True)
                start = pl.multiple_of(block * live + s * LANES, LANES)
                cauchy[pl.ds(start, LANES), :] = value.astype(jnp.bfloat16)
        return squares

    squares = jnp.zeros((1, live), jnp.float32)
    if device_total <= 8:
        for t in range(device_total // group):
            squares = cauchy_group(t, squares)
    else:
        squares = lax.fori_loop(0, device_total // group, cauchy_group, squares)
    scale = 1.0 / jnp.sqrt(squares)

    def product(owner, k):
        start = pl.multiple_of(owner * live, live)
        return jnp.dot(
            panel[owner, pl.ds(k * size, size)], cauchy[pl.ds(start, live), :],
            preferred_element_type=jnp.float32,
        )

    def near(pc):
        return (
            [owner_of(x, pc, fine)]
            + [owner_of(x_of(i), pc, fine) for i in range(n_x - 1)]
            + [owner_of(x, pc, f_of(j)) for j in range(n_fine - 1)]
        )

    crossings = (n_x - 1) * (n_fine - 1)

    def spread(total_steps, body):
        repeat(total_steps, lambda n: body(n // (n_fine - 1), n % (n_fine - 1)))

    def add(owners, k, fresh=False):
        part = pl.ds(k * size, size)
        value = None if fresh else total[part]
        for owner in owners:
            term = product(owner, k)
            value = term if value is None else value + term
        total[part] = value

    def add_near_other(k):
        for owner in near(other_core):
            arrived(owner, k)
        add(near(other_core), k)

    for k in range(pieces):
        for owner in near(core)[1:]:
            arrived(owner, k)
            to_partner(owner, k)
        spread(crossings, lambda i, j: cross_send(i, j, k).start())
        if k == 0:
            for r in range(pieces):
                part = pl.ds(r * size, size)
                out[part, live:] = jnp.dot(
                    eig[part], select[:, live:], preferred_element_type=jnp.float32
                ).astype(jnp.bfloat16)
        add(near(core), k, fresh=True)
        if k >= 1:
            add_near_other(k - 1)

    retain = lax.broadcasted_iota(jnp.int32, (1, live), 1) < counts[me]

    def finish(k):
        part = pl.ds(k * size, size)

        def last(i, j):
            owner = owner_of(x_of(i), other_core, f_of(j))
            arrived(owner, k)
            add([owner], k)

        spread(crossings, last)
        updated = total[part] * scale
        kept = panel[me, part].astype(jnp.float32)
        out[part, :live] = jnp.where(retain, updated, kept).astype(jnp.bfloat16)

    for k in range(pieces):
        def relay(i, j):
            owner = owner_of(x_of(i), core, f_of(j))
            arrived(owner, k)
            to_partner(owner, k)

        spread(crossings, relay)
        if k == 0:
            add_near_other(pieces - 1)
        spread(crossings, lambda i, j: add([owner_of(x_of(i), core, f_of(j))], k))
        if k >= 1:
            finish(k - 1)
    finish(pieces - 1)

    for k in range(pieces):
        for copy in own_sends(k):
            copy.wait_send()
        for owner in near(core)[1:]:
            send(owner, k, partner_sem.at[owner, k], partner).wait_send()

        def drain(i, j):
            cross_send(i, j, k).wait_send()
            owner = owner_of(x_of(i), core, f_of(j))
            send(owner, k, partner_sem.at[owner, k], partner).wait_send()

        spread(crossings, drain)


def per_device(n_coarse, n_fine, eigvecs, perm, counts, poles, weights, roots):
    rows, columns = eigvecs.shape
    live = UNDEF_MOST
    device_total = n_coarse * n_fine
    pieces = 4 if device_total <= 8 else 2
    hops = n_coarse // CORES - 1 + n_fine - 1
    crossings = max(1, (n_coarse // CORES - 1) * (n_fine - 1))
    lanes = lambda v: v.reshape(-1, LANES)
    operands = [eigvecs, lanes(perm), counts, lanes(poles), lanes(weights), lanes(roots)]
    anywhere = pl.BlockSpec(memory_space=pltpu.HBM)
    return pl.pallas_call(
        functools.partial(merge_kernel, n_coarse, n_fine, pieces),
        out_shape=jax.ShapeDtypeStruct((rows, columns), jnp.bfloat16),
        in_specs=[anywhere] * 6,
        out_specs=pl.BlockSpec(memory_space=pltpu.VMEM),
        scratch_shapes=[
            pltpu.VMEM((rows, columns), jnp.bfloat16),
            pltpu.VMEM((columns // LANES, LANES), jnp.int32),
            pltpu.SMEM((device_total,), jnp.int32),
            pltpu.VMEM((device_total * columns // LANES, LANES), jnp.float32),
            pltpu.VMEM((device_total * columns // LANES, LANES), jnp.float32),
            pltpu.VMEM((columns // LANES, LANES), jnp.float32),
            pltpu.VMEM((columns, columns), jnp.bfloat16),
            pltpu.VMEM((device_total, rows, live), jnp.bfloat16),
            pltpu.VMEM((device_total * live, live), jnp.bfloat16),
            pltpu.VMEM((rows, live), jnp.float32),
            pltpu.SemaphoreType.DMA((pieces,)),
            pltpu.SemaphoreType.DMA((5,)),
            pltpu.SemaphoreType.DMA((device_total, pieces)),
            pltpu.SemaphoreType.DMA((hops, pieces)),
            pltpu.SemaphoreType.DMA((device_total, pieces)),
            pltpu.SemaphoreType.DMA((crossings, pieces)),
        ],
        compiler_params=pltpu.CompilerParams(
            collective_id=0, has_side_effects=True, vmem_limit_bytes=48 * 2**20
        ),
        name="merge",
    )(*[pltpu.with_memory_space_constraint(v, pltpu.HBM) for v in operands])


def solution(mesh):
    in_specs = (
        P("rows", ("coarse", "fine")),
        P(("coarse", "fine")),
        P(),
        P(),
        P(),
        P(("coarse", "fine")),
    )
    out_specs = P("rows", ("coarse", "fine"))
    body = functools.partial(per_device, mesh.shape["coarse"], mesh.shape["fine"])
    return jax.shard_map(
        body, mesh=mesh, in_specs=in_specs, out_specs=out_specs, check_vma=False
    )
```

```python
import functools

import jax
import jax.numpy as jnp
from jax import lax
from jax.experimental import pallas as pl
from jax.experimental.pallas import tpu as pltpu
from jax.sharding import PartitionSpec as P

UNDEF_MOST = 256
LANES = 128
CORES = 2
MESH = pl.DeviceIdType.MESH


def repeat(total, body):
    if total <= 8:
        for i in range(total):
            body(i)
    else:
        lax.fori_loop(0, total, lambda i, c: (body(i), c)[1], 0)


def merge_kernel(
    n_coarse, n_fine, pieces, eig_hbm, perm_hbm, counts_hbm, poles_hbm, weights_hbm, roots_hbm, out,
    eig, perm, counts, poles, weights, roots, select, panel, cauchy, total,
    in_sem, small_sem, recv_sem, own_sem, partner_sem, cross_sem,
):
    rows, columns = eig.shape
    live = UNDEF_MOST
    device_total = n_coarse * n_fine
    n_x = n_coarse // CORES
    size = rows // pieces
    coarse = lax.axis_index("coarse")
    fine = lax.axis_index("fine")
    x = coarse // CORES
    core = lax.rem(coarse, CORES)
    other_core = 1 - core

    def owner_of(px, pc, pf):
        return (px * CORES + pc) * n_fine + pf

    def device_of(px, pc, pf):
        return {"coarse": px * CORES + pc, "fine": pf}

    me = owner_of(x, core, fine)
    x_of = lambda i: lax.rem(x + 1 + i, n_x)
    f_of = lambda j: lax.rem(fine + 1 + j, n_fine)
    partner = device_of(x, other_core, fine)

    barrier = pltpu.get_barrier_semaphore()
    pl.semaphore_signal(barrier, inc=1, device_id=partner, device_id_type=MESH)
    for i in range(n_x - 1):
        pl.semaphore_signal(barrier, inc=1, device_id=device_of(x_of(i), core, fine), device_id_type=MESH)
    for j in range(n_fine - 1):
        pl.semaphore_signal(barrier, inc=1, device_id=device_of(x, core, f_of(j)), device_id_type=MESH)

    perm_in = pltpu.make_async_copy(perm_hbm, perm, small_sem.at[0])
    perm_in.start()
    eig_in = []
    for k in range(pieces):
        part = pl.ds(k * size, size)
        copy = pltpu.make_async_copy(eig_hbm.at[part], eig.at[part], in_sem.at[k])
        copy.start()
        eig_in.append(copy)
    small_in = [
        pltpu.make_async_copy(counts_hbm, counts, small_sem.at[1]),
        pltpu.make_async_copy(poles_hbm, poles, small_sem.at[2]),
        pltpu.make_async_copy(weights_hbm, weights, small_sem.at[3]),
        pltpu.make_async_copy(roots_hbm, roots, small_sem.at[4]),
    ]
    for copy in small_in:
        copy.start()

    def send(owner, k, sem, target):
        part = panel.at[owner, pl.ds(k * size, size)]
        return pltpu.make_async_remote_copy(
            src_ref=part, dst_ref=part, send_sem=sem, recv_sem=recv_sem.at[owner, k],
            device_id=target, device_id_type=MESH,
        )

    def arrived(owner, k):
        send(owner, k, partner_sem.at[owner, k], partner).wait_recv()

    def to_partner(owner, k):
        send(owner, k, partner_sem.at[owner, k], partner).start()

    n_lead, n_trail = n_fine - 1, n_x - 1
    balanced = n_lead == n_trail

    def choose(k, a, b):
        return jnp.where(core == k % CORES, a, b) if balanced else a

    def lead_owner(j, k):
        return choose(k, owner_of(x, core, f_of(j)), owner_of(x_of(j), core, fine))

    def trail_owner(i, k):
        return choose(k, owner_of(x_of(i), core, fine), owner_of(x, core, f_of(i)))

    def lead_target(j, k):
        return {"coarse": choose(k, x, x_of(j)) * CORES + core, "fine": choose(k, f_of(j), fine)}

    def trail_target(i, k):
        return {"coarse": choose(k, x_of(i), x) * CORES + core, "fine": choose(k, fine, f_of(i))}

    def lead_send(j, k):
        return send(me, k, own_sem.at[j, k], lead_target(j, k))

    def trail_send(i, k):
        return send(me, k, own_sem.at[n_lead + i, k], trail_target(i, k))

    def cross_send(i, j, k):
        return send(lead_owner(j, k), k, cross_sem.at[i * n_lead + j, k], trail_target(i, k))

    def early_sends(k):
        for j in range(n_lead):
            lead_send(j, k).start()
        to_partner(me, k)

    def build_select(low, high):
        source = lax.broadcasted_iota(jnp.int32, (columns, LANES), 0)
        for q in range(low // LANES, high // LANES):
            hit = source == perm[q : q + 1, :]
            select[:, q * LANES : (q + 1) * LANES] = jnp.where(hit, 1.0, 0.0).astype(jnp.bfloat16)

    perm_in.wait()
    build_select(0, live)

    for k in range(pieces):
        part = pl.ds(k * size, size)
        eig_in[k].wait()
        panel[me, part] = jnp.dot(
            eig[part], select[:, :live], preferred_element_type=jnp.float32
        ).astype(jnp.bfloat16)
        if k == 0:
            pl.semaphore_wait(barrier, n_x + n_fine - 1)
            early_sends(0)
        elif k >= 2:
            early_sends(k - 1)
    for copy in small_in:
        copy.wait()
    if pieces > 1:
        early_sends(pieces - 1)

    width = columns // LANES
    group = 8 // width
    root_row = jnp.concatenate([roots[s : s + 1, :] for s in range(live // LANES)], axis=1)
    within = lax.broadcasted_iota(jnp.int32, (LANES, 1), 0)

    def cauchy_group(t, squares):
        lines = pl.ds(pl.multiple_of(t * 8, 8), 8)
        pole_t = jnp.transpose(poles[lines, :])
        weight_t = jnp.transpose(weights[lines, :])
        for h in range(group):
            block = t * group + h
            count = counts[block]
            for s in range(live // LANES):
                at = h * width + s
                alive = within + s * LANES < count
                factor = jnp.where(alive, weight_t[:, at : at + 1], 0.0)
                value = factor / (pole_t[:, at : at + 1] - root_row)
                squares = squares + jnp.sum(value * value, axis=0, keepdims=True)
                start = pl.multiple_of(block * live + s * LANES, LANES)
                cauchy[pl.ds(start, LANES), :] = value.astype(jnp.bfloat16)
        return squares

    squares = jnp.zeros((1, live), jnp.float32)
    if device_total <= 8:
        for t in range(device_total // group):
            squares = cauchy_group(t, squares)
    else:
        squares = lax.fori_loop(0, device_total // group, cauchy_group, squares)
    scale = 1.0 / jnp.sqrt(squares)

    def product(owner, k):
        start = pl.multiple_of(owner * live, live)
        return jnp.dot(
            panel[owner, pl.ds(k * size, size)], cauchy[pl.ds(start, live), :],
            preferred_element_type=jnp.float32,
        )

    crossings = n_lead * n_trail

    def spread(total_steps, body):
        repeat(total_steps, lambda n: body(n // (n_fine - 1), n % (n_fine - 1)))

    def add(owners, k, fresh=False):
        part = pl.ds(k * size, size)
        value = None if fresh else total[part]
        for owner in owners:
            term = product(owner, k)
            value = term if value is None else value + term
        total[part] = value

    def near_group(pc, k, fresh=False):
        add([owner_of(x, pc, fine)] + [lead_owner_of(pc, j, k) for j in range(n_lead)], k, fresh)

    def lead_owner_of(pc, j, k):
        if pc is core or not balanced:
            return pc_owner(lead_owner(j, k), pc)
        return pc_owner(trail_owner(j, k), pc)

    def trail_owner_of(pc, i, k):
        if pc is core or not balanced:
            return pc_owner(trail_owner(i, k), pc)
        return pc_owner(lead_owner(i, k), pc)

    def pc_owner(owner, pc):
        return owner if pc is core else owner + (pc - core) * n_fine

    def far_owner(pc, i, j):
        return owner_of(x_of(i), pc, f_of(j))

    for k in range(pieces):
        for j in range(n_lead):
            arrived(lead_owner(j, k), k)
            for i in range(n_trail):
                trail_send(i, k).start() if j == 0 else None
                cross_send(i, j, k).start()
            to_partner(lead_owner(j, k), k)
        if k == 0:
            build_select(live, columns)
            for r in range(pieces):
                part = pl.ds(r * size, size)
                out[part, live:] = jnp.dot(
                    eig[part], select[:, live:], preferred_element_type=jnp.float32
                ).astype(jnp.bfloat16)
        near_group(core, k, fresh=True)

    retain = lax.broadcasted_iota(jnp.int32, (1, live), 1) < counts[me]

    def finish(k):
        part = pl.ds(k * size, size)
        for i in range(n_trail):
            arrived(trail_owner_of(other_core, i, k), k)
        if n_trail > 0:
            add([trail_owner_of(other_core, i, k) for i in range(n_trail)], k)

        def last(i, j):
            owner = far_owner(other_core, i, j)
            arrived(owner, k)
            add([owner], k)

        spread(crossings, last)
        updated = total[part] * scale
        kept = panel[me, part].astype(jnp.float32)
        out[part, :live] = jnp.where(retain, updated, kept).astype(jnp.bfloat16)

    for k in range(pieces):
        for i in range(n_trail):
            arrived(trail_owner(i, k), k)
            to_partner(trail_owner(i, k), k)

        def relay(i, j):
            arrived(far_owner(core, i, j), k)
            to_partner(far_owner(core, i, j), k)

        spread(crossings, relay)
        arrived(owner_of(x, other_core, fine), k)
        for j in range(n_lead):
            arrived(lead_owner_of(other_core, j, k), k)
        near_group(other_core, k)
        if n_trail > 0:
            add([trail_owner(i, k) for i in range(n_trail)], k)
        spread(crossings, lambda i, j: add([far_owner(core, i, j)], k))
        if k >= 1:
            finish(k - 1)
    finish(pieces - 1)

    for k in range(pieces):
        for j in range(n_lead):
            lead_send(j, k).wait_send()
            send(lead_owner(j, k), k, partner_sem.at[lead_owner(j, k), k], partner).wait_send()
        for i in range(n_trail):
            trail_send(i, k).wait_send()
            send(trail_owner(i, k), k, partner_sem.at[trail_owner(i, k), k], partner).wait_send()
        send(me, k, partner_sem.at[me, k], partner).wait_send()

        def drain(i, j):
            cross_send(i, j, k).wait_send()
            owner = far_owner(core, i, j)
            send(owner, k, partner_sem.at[owner, k], partner).wait_send()

        spread(crossings, drain)


def per_device(n_coarse, n_fine, eigvecs, perm, counts, poles, weights, roots):
    rows, columns = eigvecs.shape
    live = UNDEF_MOST
    device_total = n_coarse * n_fine
    pieces = 4 if device_total <= 8 else 2
    hops = n_coarse // CORES - 1 + n_fine - 1
    crossings = max(1, (n_coarse // CORES - 1) * (n_fine - 1))
    lanes = lambda v: v.reshape(-1, LANES)
    operands = [eigvecs, lanes(perm), counts, lanes(poles), lanes(weights), lanes(roots)]
    anywhere = pl.BlockSpec(memory_space=pltpu.HBM)
    return pl.pallas_call(
        functools.partial(merge_kernel, n_coarse, n_fine, pieces),
        out_shape=jax.ShapeDtypeStruct((rows, columns), jnp.bfloat16),
        in_specs=[anywhere] * 6,
        out_specs=pl.BlockSpec(memory_space=pltpu.VMEM),
        scratch_shapes=[
            pltpu.VMEM((rows, columns), jnp.bfloat16),
            pltpu.VMEM((columns // LANES, LANES), jnp.int32),
            pltpu.SMEM((device_total,), jnp.int32),
            pltpu.VMEM((device_total * columns // LANES, LANES), jnp.float32),
            pltpu.VMEM((device_total * columns // LANES, LANES), jnp.float32),
            pltpu.VMEM((columns // LANES, LANES), jnp.float32),
            pltpu.VMEM((columns, columns), jnp.bfloat16),
            pltpu.VMEM((device_total, rows, live), jnp.bfloat16),
            pltpu.VMEM((device_total * live, live), jnp.bfloat16),
            pltpu.VMEM((rows, live), jnp.float32),
            pltpu.SemaphoreType.DMA((pieces,)),
            pltpu.SemaphoreType.DMA((5,)),
            pltpu.SemaphoreType.DMA((device_total, pieces)),
            pltpu.SemaphoreType.DMA((hops, pieces)),
            pltpu.SemaphoreType.DMA((device_total, pieces)),
            pltpu.SemaphoreType.DMA((crossings, pieces)),
        ],
        compiler_params=pltpu.CompilerParams(
            collective_id=0, has_side_effects=True, vmem_limit_bytes=48 * 2**20
        ),
        name="merge",
    )(*[pltpu.with_memory_space_constraint(v, pltpu.HBM) for v in operands])


def solution(mesh):
    in_specs = (
        P("rows", ("coarse", "fine")),
        P(("coarse", "fine")),
        P(),
        P(),
        P(),
        P(("coarse", "fine")),
    )
    out_specs = P("rows", ("coarse", "fine"))
    body = functools.partial(per_device, mesh.shape["coarse"], mesh.shape["fine"])
    return jax.shard_map(
        body, mesh=mesh, in_specs=in_specs, out_specs=out_specs, check_vma=False
    )
```

```python
import functools

import jax
import jax.numpy as jnp
from jax import lax
from jax.experimental import pallas as pl
from jax.experimental.pallas import tpu as pltpu
from jax.sharding import PartitionSpec as P

UNDEF_MOST = 256
LANES = 128
CORES = 2
MESH = pl.DeviceIdType.MESH


def repeat(total, body):
    if total <= 8:
        for i in range(total):
            body(i)
    else:
        lax.fori_loop(0, total, lambda i, c: (body(i), c)[1], 0)


def merge_kernel(
    n_coarse, n_fine, pieces, eig_hbm, perm_hbm, counts_hbm, poles_hbm, weights_hbm, roots_hbm, out,
    eig, perm, counts, poles, weights, roots, select, panel, cauchy, total,
    peer_roots, peer_cauchy, partial, incoming,
    in_sem, small_sem, recv_sem, own_sem, partner_sem, sum_send_sem, sum_recv_sem, root_send_sem, root_recv_sem,
):
    rows, columns = eig.shape
    live = UNDEF_MOST
    device_total = n_coarse * n_fine
    n_x = n_coarse // CORES
    size = rows // pieces
    coarse = lax.axis_index("coarse")
    fine = lax.axis_index("fine")
    x = coarse // CORES
    core = lax.rem(coarse, CORES)
    other_core = 1 - core

    def owner_of(px, pc, pf):
        return (px * CORES + pc) * n_fine + pf

    def device_of(px, pc, pf):
        return {"coarse": px * CORES + pc, "fine": pf}

    me = owner_of(x, core, fine)
    x_of = lambda i: lax.rem(x + 1 + i, n_x)
    f_of = lambda j: lax.rem(fine + 1 + j, n_fine)
    partner = device_of(x, other_core, fine)

    barrier = pltpu.get_barrier_semaphore()
    pl.semaphore_signal(barrier, inc=1, device_id=partner, device_id_type=MESH)
    for i in range(n_x - 1):
        pl.semaphore_signal(barrier, inc=1, device_id=device_of(x_of(i), core, fine), device_id_type=MESH)
    for j in range(n_fine - 1):
        pl.semaphore_signal(barrier, inc=1, device_id=device_of(x, core, f_of(j)), device_id_type=MESH)

    perm_in = pltpu.make_async_copy(perm_hbm, perm, small_sem.at[0])
    perm_in.start()
    eig_in = []
    for k in range(pieces):
        part = pl.ds(k * size, size)
        copy = pltpu.make_async_copy(eig_hbm.at[part], eig.at[part], in_sem.at[k])
        copy.start()
        eig_in.append(copy)
    small_in = [
        pltpu.make_async_copy(counts_hbm, counts, small_sem.at[1]),
        pltpu.make_async_copy(poles_hbm, poles, small_sem.at[2]),
        pltpu.make_async_copy(weights_hbm, weights, small_sem.at[3]),
    ]
    roots_in = pltpu.make_async_copy(roots_hbm, roots, small_sem.at[4])
    roots_in.start()
    for copy in small_in:
        copy.start()

    def send(owner, k, sem, target):
        part = panel.at[owner, pl.ds(k * size, size)]
        return pltpu.make_async_remote_copy(
            src_ref=part, dst_ref=part, send_sem=sem, recv_sem=recv_sem.at[owner, k],
            device_id=target, device_id_type=MESH,
        )

    def arrived(owner, k):
        send(owner, k, partner_sem.at[owner, k], partner).wait_recv()

    def to_partner(owner, k):
        send(owner, k, partner_sem.at[owner, k], partner).start()

    balanced = n_x == n_fine
    over_fine = lambda k: not balanced or k % 2 == 0
    x_peers = [(x_of(i), fine) for i in range(n_x - 1)]
    f_peers = [(x, f_of(j)) for j in range(n_fine - 1)]

    def gather_peers(k):
        return f_peers if over_fine(k) else x_peers

    def sum_peers(k):
        return x_peers if over_fine(k) else f_peers

    def peer_owner(peer, pc):
        return owner_of(peer[0], pc, peer[1])

    def gather_send(n, k):
        px, pf = gather_peers(k)[n]
        return send(me, k, own_sem.at[n, k], device_of(px, core, pf))

    def early_sends(k):
        for n in range(len(gather_peers(k))):
            gather_send(n, k).start()
        to_partner(me, k)

    def sum_send(n, k):
        part = pl.ds(k * size, size)
        peers = sum_peers(k)
        px, pf = peers[n]
        slot = len(peers) - 1 - n
        return pltpu.make_async_remote_copy(
            src_ref=partial.at[n, part], dst_ref=incoming.at[slot, part],
            send_sem=sum_send_sem.at[n, k], recv_sem=sum_recv_sem.at[slot, k],
            device_id=device_of(px, core, pf), device_id_type=MESH,
        )

    root_peers = x_peers + (f_peers if balanced else [])

    def root_send(n):
        px, pf = root_peers[n]
        base, count = (0, n_x - 1) if n < n_x - 1 else (n_x - 1, n_fine - 1)
        slot = base + count - 1 - (n - base)
        return pltpu.make_async_remote_copy(
            src_ref=roots, dst_ref=peer_roots.at[slot],
            send_sem=root_send_sem.at[n], recv_sem=root_recv_sem.at[slot],
            device_id=device_of(px, core, pf), device_id_type=MESH,
        )

    def build_select(low, high):
        source = lax.broadcasted_iota(jnp.int32, (columns, LANES), 0)
        for q in range(low // LANES, high // LANES):
            hit = source == perm[q : q + 1, :]
            select[:, q * LANES : (q + 1) * LANES] = jnp.where(hit, 1.0, 0.0).astype(jnp.bfloat16)

    perm_in.wait()
    build_select(0, live)

    for k in range(pieces):
        part = pl.ds(k * size, size)
        eig_in[k].wait()
        panel[me, part] = jnp.dot(
            eig[part], select[:, :live], preferred_element_type=jnp.float32
        ).astype(jnp.bfloat16)
        if k == 0:
            pl.semaphore_wait(barrier, n_x + n_fine - 1)
            roots_in.wait()
            for n in range(len(root_peers)):
                root_send(n).start()
            early_sends(0)
        elif k >= 2:
            early_sends(k - 1)
    for copy in small_in:
        copy.wait()
    if pieces > 1:
        early_sends(pieces - 1)

    width = columns // LANES
    group = 8 // width
    as_row = lambda v: jnp.concatenate([v[n : n + 1, :] for n in range(live // LANES)], axis=1)
    root_row = as_row(roots)
    within = lax.broadcasted_iota(jnp.int32, (LANES, 1), 0)

    def cauchy_group(t, squares):
        lines = pl.ds(pl.multiple_of(t * 8, 8), 8)
        pole_t = jnp.transpose(poles[lines, :])
        weight_t = jnp.transpose(weights[lines, :])
        for h in range(group):
            block = t * group + h
            count = counts[block]
            for s in range(live // LANES):
                at = h * width + s
                alive = within + s * LANES < count
                factor = jnp.where(alive, weight_t[:, at : at + 1], 0.0)
                value = factor / (pole_t[:, at : at + 1] - root_row)
                squares = squares + jnp.sum(value * value, axis=0, keepdims=True)
                start = pl.multiple_of(block * live + s * LANES, LANES)
                cauchy[pl.ds(start, LANES), :] = value.astype(jnp.bfloat16)
        return squares

    def peer_block(slot, row, block):
        lines = pl.ds(pl.multiple_of(block // group * 8, 8), 8)
        pole_t = jnp.transpose(poles[lines, :])
        weight_t = jnp.transpose(weights[lines, :])
        h = lax.rem(block, group)
        count = counts[block]
        for s in range(live // LANES):
            pole, weight = pole_t[:, s : s + 1], weight_t[:, s : s + 1]
            for other in range(1, group):
                at = other * width + s
                pole = jnp.where(h == other, pole_t[:, at : at + 1], pole)
                weight = jnp.where(h == other, weight_t[:, at : at + 1], weight)
            factor = jnp.where(within + s * LANES < count, weight, 0.0)
            value = factor / (pole - row)
            start = pl.multiple_of(block * live + s * LANES, LANES)
            peer_cauchy[slot, pl.ds(start, LANES), :] = value.astype(jnp.bfloat16)

    def gathered(k, pc):
        return [owner_of(x, pc, fine)] + [peer_owner(p, pc) for p in gather_peers(k)]

    for n in range(len(root_peers)):
        root_send(n).wait_recv()
    for n in range(len(root_peers)):
        row = as_row(peer_roots.at[n])
        if n < n_x - 1:
            repeat(CORES * n_fine, lambda b: peer_block(n, row, x * CORES * n_fine + b))
        else:
            repeat(CORES * n_x, lambda b: peer_block(n, row, b * n_fine + fine))

    def product(source, owner, k):
        start = pl.multiple_of(owner * live, live)
        return jnp.dot(
            panel[owner, pl.ds(k * size, size)], source[pl.ds(start, live), :],
            preferred_element_type=jnp.float32,
        )

    def block_sum(source, k):
        value = None
        for owner in gathered(k, core) + gathered(k, other_core):
            term = product(source, owner, k)
            value = term if value is None else value + term
        return value

    def relay(k):
        for owner in gathered(k, core)[1:]:
            arrived(owner, k)
            to_partner(owner, k)

    def rest_piece(k):
        part = pl.ds(k * size, size)
        out[part, live:] = jnp.dot(
            eig[part], select[:, live:], preferred_element_type=jnp.float32
        ).astype(jnp.bfloat16)

    def partials(k):
        part = pl.ds(k * size, size)
        for owner in gathered(k, other_core):
            arrived(owner, k)
        base = 0 if over_fine(k) else n_x - 1
        for n in range(len(sum_peers(k))):
            partial[n, part] = block_sum(peer_cauchy.at[base + n], k).astype(jnp.bfloat16)
        rest_piece(k)
        for n in range(len(sum_peers(k))):
            sum_send(n, k).start()

    retain = lax.broadcasted_iota(jnp.int32, (1, live), 1) < counts[me]

    def finish(k):
        part = pl.ds(k * size, size)
        value = total[part]
        for n in range(len(sum_peers(k))):
            sum_send(n, k).wait_recv()
        for n in range(len(sum_peers(k))):
            value = value + incoming[n, part].astype(jnp.float32)
        updated = value * scale
        kept = panel[me, part].astype(jnp.float32)
        out[part, :live] = jnp.where(retain, updated, kept).astype(jnp.bfloat16)

    build_select(live, columns)
    ahead = min(2, pieces)
    for k in range(ahead):
        relay(k)
    for k in range(pieces):
        partials(k)
        if k + ahead < pieces:
            relay(k + ahead)
    squares = jnp.zeros((1, live), jnp.float32)
    if device_total <= 8:
        for t in range(device_total // group):
            squares = cauchy_group(t, squares)
    else:
        squares = lax.fori_loop(0, device_total // group, cauchy_group, squares)
    scale = 1.0 / jnp.sqrt(squares)

    for k in range(pieces):
        total[pl.ds(k * size, size)] = block_sum(cauchy, k)
    for k in range(pieces):
        finish(k)

    for n in range(len(root_peers)):
        root_send(n).wait_send()
    for k in range(pieces):
        for n in range(len(gather_peers(k))):
            gather_send(n, k).wait_send()
        for owner in gathered(k, core):
            send(owner, k, partner_sem.at[owner, k], partner).wait_send()
        for n in range(len(sum_peers(k))):
            sum_send(n, k).wait_send()


def per_device(n_coarse, n_fine, eigvecs, perm, counts, poles, weights, roots):
    rows, columns = eigvecs.shape
    live = UNDEF_MOST
    device_total = n_coarse * n_fine
    pieces = 4 if device_total <= 8 else 2
    n_x = n_coarse // CORES
    hops = max(n_x, n_fine) - 1
    sums = n_x - 1
    row_sets = n_x - 1 + (n_fine - 1 if n_x == n_fine else 0)
    lanes = lambda v: v.reshape(-1, LANES)
    operands = [eigvecs, lanes(perm), counts, lanes(poles), lanes(weights), lanes(roots)]
    anywhere = pl.BlockSpec(memory_space=pltpu.HBM)
    return pl.pallas_call(
        functools.partial(merge_kernel, n_coarse, n_fine, pieces),
        out_shape=jax.ShapeDtypeStruct((rows, columns), jnp.bfloat16),
        in_specs=[anywhere] * 6,
        out_specs=pl.BlockSpec(memory_space=pltpu.VMEM),
        scratch_shapes=[
            pltpu.VMEM((rows, columns), jnp.bfloat16),
            pltpu.VMEM((columns // LANES, LANES), jnp.int32),
            pltpu.SMEM((device_total,), jnp.int32),
            pltpu.VMEM((device_total * columns // LANES, LANES), jnp.float32),
            pltpu.VMEM((device_total * columns // LANES, LANES), jnp.float32),
            pltpu.VMEM((columns // LANES, LANES), jnp.float32),
            pltpu.VMEM((columns, columns), jnp.bfloat16),
            pltpu.VMEM((device_total, rows, live), jnp.bfloat16),
            pltpu.VMEM((device_total * live, live), jnp.bfloat16),
            pltpu.VMEM((rows, live), jnp.float32),
            pltpu.VMEM((row_sets, columns // LANES, LANES), jnp.float32),
            pltpu.VMEM((row_sets, device_total * live, live), jnp.bfloat16),
            pltpu.VMEM((sums, rows, live), jnp.bfloat16),
            pltpu.VMEM((sums, rows, live), jnp.bfloat16),
            pltpu.SemaphoreType.DMA((pieces,)),
            pltpu.SemaphoreType.DMA((5,)),
            pltpu.SemaphoreType.DMA((device_total, pieces)),
            pltpu.SemaphoreType.DMA((hops, pieces)),
            pltpu.SemaphoreType.DMA((device_total, pieces)),
            pltpu.SemaphoreType.DMA((sums, pieces)),
            pltpu.SemaphoreType.DMA((sums, pieces)),
            pltpu.SemaphoreType.DMA((row_sets,)),
            pltpu.SemaphoreType.DMA((row_sets,)),
        ],
        compiler_params=pltpu.CompilerParams(
            collective_id=0, has_side_effects=True, vmem_limit_bytes=48 * 2**20
        ),
        name="merge",
    )(*[pltpu.with_memory_space_constraint(v, pltpu.HBM) for v in operands])


def solution(mesh):
    in_specs = (
        P("rows", ("coarse", "fine")),
        P(("coarse", "fine")),
        P(),
        P(),
        P(),
        P(("coarse", "fine")),
    )
    out_specs = P("rows", ("coarse", "fine"))
    body = functools.partial(per_device, mesh.shape["coarse"], mesh.shape["fine"])
    return jax.shard_map(
        body, mesh=mesh, in_specs=in_specs, out_specs=out_specs, check_vma=False
    )
```

```python
import functools

import jax
import jax.numpy as jnp
from jax import lax
from jax.experimental import pallas as pl
from jax.experimental.pallas import tpu as pltpu
from jax.sharding import PartitionSpec as P

UNDEF_MOST = 256
LANES = 128
CORES = 2
MESH = pl.DeviceIdType.MESH


def repeat(total, body):
    if total <= 8:
        for i in range(total):
            body(i)
    else:
        lax.fori_loop(0, total, lambda i, c: (body(i), c)[1], 0)


def merge_kernel(
    n_coarse, n_fine, pieces, eig_hbm, perm_hbm, counts_hbm, poles_hbm, weights_hbm, roots_hbm, out,
    eig, perm, counts, poles, weights, roots, select, panel, cauchy, total,
    peer_roots, peer_cauchy, partial, incoming,
    in_sem, small_sem, recv_sem, own_sem, partner_sem, sum_send_sem, sum_recv_sem, root_send_sem, root_recv_sem,
):
    rows, columns = eig.shape
    live = UNDEF_MOST
    device_total = n_coarse * n_fine
    n_x = n_coarse // CORES
    size = rows // pieces
    coarse = lax.axis_index("coarse")
    fine = lax.axis_index("fine")
    x = coarse // CORES
    core = lax.rem(coarse, CORES)
    other_core = 1 - core

    def owner_of(px, pc, pf):
        return (px * CORES + pc) * n_fine + pf

    def device_of(px, pc, pf):
        return {"coarse": px * CORES + pc, "fine": pf}

    me = owner_of(x, core, fine)
    x_of = lambda i: lax.rem(x + 1 + i, n_x)
    f_of = lambda j: lax.rem(fine + 1 + j, n_fine)
    partner = device_of(x, other_core, fine)

    barrier = pltpu.get_barrier_semaphore()
    pl.semaphore_signal(barrier, inc=1, device_id=partner, device_id_type=MESH)
    for i in range(n_x - 1):
        pl.semaphore_signal(barrier, inc=1, device_id=device_of(x_of(i), core, fine), device_id_type=MESH)
    for j in range(n_fine - 1):
        pl.semaphore_signal(barrier, inc=1, device_id=device_of(x, core, f_of(j)), device_id_type=MESH)

    perm_in = pltpu.make_async_copy(perm_hbm, perm, small_sem.at[0])
    perm_in.start()
    eig_in = []
    for k in range(pieces):
        part = pl.ds(k * size, size)
        copy = pltpu.make_async_copy(eig_hbm.at[part], eig.at[part], in_sem.at[k])
        copy.start()
        eig_in.append(copy)
    small_in = [
        pltpu.make_async_copy(counts_hbm, counts, small_sem.at[1]),
        pltpu.make_async_copy(poles_hbm, poles, small_sem.at[2]),
        pltpu.make_async_copy(weights_hbm, weights, small_sem.at[3]),
    ]
    roots_in = pltpu.make_async_copy(roots_hbm, roots, small_sem.at[4])
    roots_in.start()
    for copy in small_in:
        copy.start()

    def send(owner, k, sem, target):
        part = panel.at[owner, pl.ds(k * size, size)]
        return pltpu.make_async_remote_copy(
            src_ref=part, dst_ref=part, send_sem=sem, recv_sem=recv_sem.at[owner, k],
            device_id=target, device_id_type=MESH,
        )

    def arrived(owner, k):
        send(owner, k, partner_sem.at[owner, k], partner).wait_recv()

    def to_partner(owner, k):
        send(owner, k, partner_sem.at[owner, k], partner).start()

    balanced = n_x == n_fine
    over_fine = lambda k: not balanced or k % 2 == 0
    x_peers = [(x_of(i), fine) for i in range(n_x - 1)]
    f_peers = [(x, f_of(j)) for j in range(n_fine - 1)]

    def gather_peers(k):
        return f_peers if over_fine(k) else x_peers

    def sum_peers(k):
        return x_peers if over_fine(k) else f_peers

    def peer_owner(peer, pc):
        return owner_of(peer[0], pc, peer[1])

    def gather_send(n, k):
        px, pf = gather_peers(k)[n]
        return send(me, k, own_sem.at[n, k], device_of(px, core, pf))

    def early_sends(k):
        for n in range(len(gather_peers(k))):
            gather_send(n, k).start()
        to_partner(me, k)

    def sum_send(n, k):
        part = pl.ds(k * size, size)
        peers = sum_peers(k)
        px, pf = peers[n]
        slot = len(peers) - 1 - n
        return pltpu.make_async_remote_copy(
            src_ref=partial.at[n, part], dst_ref=incoming.at[slot, part],
            send_sem=sum_send_sem.at[n, k], recv_sem=sum_recv_sem.at[slot, k],
            device_id=device_of(px, core, pf), device_id_type=MESH,
        )

    root_peers = x_peers + (f_peers if balanced else [])

    def root_send(n):
        px, pf = root_peers[n]
        base, count = (0, n_x - 1) if n < n_x - 1 else (n_x - 1, n_fine - 1)
        slot = base + count - 1 - (n - base)
        return pltpu.make_async_remote_copy(
            src_ref=roots, dst_ref=peer_roots.at[slot],
            send_sem=root_send_sem.at[n], recv_sem=root_recv_sem.at[slot],
            device_id=device_of(px, core, pf), device_id_type=MESH,
        )

    def build_select(low, high):
        source = lax.broadcasted_iota(jnp.int32, (columns, LANES), 0)
        for q in range(low // LANES, high // LANES):
            hit = source == perm[q : q + 1, :]
            select[:, q * LANES : (q + 1) * LANES] = jnp.where(hit, 1.0, 0.0).astype(jnp.bfloat16)

    perm_in.wait()
    build_select(0, live)

    for k in range(pieces):
        part = pl.ds(k * size, size)
        eig_in[k].wait()
        panel[me, part] = jnp.dot(
            eig[part], select[:, :live], preferred_element_type=jnp.float32
        ).astype(jnp.bfloat16)
        if k == 0:
            pl.semaphore_wait(barrier, n_x + n_fine - 1)
            roots_in.wait()
            for n in range(len(root_peers)):
                root_send(n).start()
            early_sends(0)
        elif k >= 2:
            early_sends(k - 1)
    for copy in small_in:
        copy.wait()
    if pieces > 1:
        early_sends(pieces - 1)

    width = columns // LANES
    group = 8 // width
    as_row = lambda v: jnp.concatenate([v[n : n + 1, :] for n in range(live // LANES)], axis=1)
    root_row = as_row(roots)
    within = lax.broadcasted_iota(jnp.int32, (LANES, 1), 0)

    def cauchy_group(t, squares):
        lines = pl.ds(pl.multiple_of(t * 8, 8), 8)
        pole_t = jnp.transpose(poles[lines, :])
        weight_t = jnp.transpose(weights[lines, :])
        for h in range(group):
            block = t * group + h
            count = counts[block]
            for s in range(live // LANES):
                at = h * width + s
                alive = within + s * LANES < count
                factor = jnp.where(alive, weight_t[:, at : at + 1], 0.0)
                value = factor / (pole_t[:, at : at + 1] - root_row)
                squares = squares + jnp.sum(value * value, axis=0, keepdims=True)
                start = pl.multiple_of(block * live + s * LANES, LANES)
                cauchy[pl.ds(start, LANES), :] = value.astype(jnp.bfloat16)
        return squares

    def peer_block(slot, row, block):
        lines = pl.ds(pl.multiple_of(block // group * 8, 8), 8)
        pole_t = jnp.transpose(poles[lines, :])
        weight_t = jnp.transpose(weights[lines, :])
        h = lax.rem(block, group)
        count = counts[block]
        for s in range(live // LANES):
            pole, weight = pole_t[:, s : s + 1], weight_t[:, s : s + 1]
            for other in range(1, group):
                at = other * width + s
                pole = jnp.where(h == other, pole_t[:, at : at + 1], pole)
                weight = jnp.where(h == other, weight_t[:, at : at + 1], weight)
            factor = jnp.where(within + s * LANES < count, weight, 0.0)
            value = factor / (pole - row)
            start = pl.multiple_of(block * live + s * LANES, LANES)
            peer_cauchy[slot, pl.ds(start, LANES), :] = value.astype(jnp.bfloat16)

    def gathered(k, pc):
        return [owner_of(x, pc, fine)] + [peer_owner(p, pc) for p in gather_peers(k)]

    build_select(live, columns)
    for n in range(len(root_peers)):
        root_send(n).wait_recv()
    def peer_panel(n):
        row = as_row(peer_roots.at[n])
        if n < n_x - 1:
            repeat(CORES * n_fine, lambda b: peer_block(n, row, x * CORES * n_fine + b))
        else:
            repeat(CORES * n_x, lambda b: peer_block(n, row, b * n_fine + fine))

    for n in range(n_x - 1):
        peer_panel(n)

    def product(source, owner, k):
        start = pl.multiple_of(owner * live, live)
        return jnp.dot(
            panel[owner, pl.ds(k * size, size)], source[pl.ds(start, live), :],
            preferred_element_type=jnp.float32,
        )

    def block_sum(source, k):
        value = None
        for owner in gathered(k, core) + gathered(k, other_core):
            term = product(source, owner, k)
            value = term if value is None else value + term
        return value

    def relay(k):
        for owner in gathered(k, core)[1:]:
            arrived(owner, k)
            to_partner(owner, k)

    def rest_piece(k):
        part = pl.ds(k * size, size)
        out[part, live:] = jnp.dot(
            eig[part], select[:, live:], preferred_element_type=jnp.float32
        ).astype(jnp.bfloat16)

    def partials(k):
        part = pl.ds(k * size, size)
        for owner in gathered(k, other_core):
            arrived(owner, k)
        base = 0 if over_fine(k) else n_x - 1
        for n in range(len(sum_peers(k))):
            partial[n, part] = block_sum(peer_cauchy.at[base + n], k).astype(jnp.bfloat16)
        rest_piece(k)
        for n in range(len(sum_peers(k))):
            sum_send(n, k).start()

    retain = lax.broadcasted_iota(jnp.int32, (1, live), 1) < counts[me]

    def finish(k):
        part = pl.ds(k * size, size)
        value = total[part]
        for n in range(len(sum_peers(k))):
            sum_send(n, k).wait_recv()
        for n in range(len(sum_peers(k))):
            value = value + incoming[n, part].astype(jnp.float32)
        updated = value * scale
        kept = panel[me, part].astype(jnp.float32)
        out[part, :live] = jnp.where(retain, updated, kept).astype(jnp.bfloat16)

    ahead = min(4, pieces)
    for k in range(ahead):
        relay(k)
    for n in range(n_x - 1, len(root_peers)):
        peer_panel(n)
    for k in range(pieces):
        partials(k)
        if k + ahead < pieces:
            relay(k + ahead)
    squares = jnp.zeros((1, live), jnp.float32)
    if device_total <= 8:
        for t in range(device_total // group):
            squares = cauchy_group(t, squares)
    else:
        squares = lax.fori_loop(0, device_total // group, cauchy_group, squares)
    scale = 1.0 / jnp.sqrt(squares)

    for k in range(pieces):
        total[pl.ds(k * size, size)] = block_sum(cauchy, k)
    for k in range(pieces):
        finish(k)

    for n in range(len(root_peers)):
        root_send(n).wait_send()
    for k in range(pieces):
        for n in range(len(gather_peers(k))):
            gather_send(n, k).wait_send()
        for owner in gathered(k, core):
            send(owner, k, partner_sem.at[owner, k], partner).wait_send()
        for n in range(len(sum_peers(k))):
            sum_send(n, k).wait_send()


def per_device(n_coarse, n_fine, eigvecs, perm, counts, poles, weights, roots):
    rows, columns = eigvecs.shape
    live = UNDEF_MOST
    device_total = n_coarse * n_fine
    pieces = 4 if device_total <= 8 else 2
    n_x = n_coarse // CORES
    hops = max(n_x, n_fine) - 1
    sums = n_x - 1
    row_sets = n_x - 1 + (n_fine - 1 if n_x == n_fine else 0)
    lanes = lambda v: v.reshape(-1, LANES)
    operands = [eigvecs, lanes(perm), counts, lanes(poles), lanes(weights), lanes(roots)]
    anywhere = pl.BlockSpec(memory_space=pltpu.HBM)
    return pl.pallas_call(
        functools.partial(merge_kernel, n_coarse, n_fine, pieces),
        out_shape=jax.ShapeDtypeStruct((rows, columns), jnp.bfloat16),
        in_specs=[anywhere] * 6,
        out_specs=pl.BlockSpec(memory_space=pltpu.VMEM),
        scratch_shapes=[
            pltpu.VMEM((rows, columns), jnp.bfloat16),
            pltpu.VMEM((columns // LANES, LANES), jnp.int32),
            pltpu.SMEM((device_total,), jnp.int32),
            pltpu.VMEM((device_total * columns // LANES, LANES), jnp.float32),
            pltpu.VMEM((device_total * columns // LANES, LANES), jnp.float32),
            pltpu.VMEM((columns // LANES, LANES), jnp.float32),
            pltpu.VMEM((columns, columns), jnp.bfloat16),
            pltpu.VMEM((device_total, rows, live), jnp.bfloat16),
            pltpu.VMEM((device_total * live, live), jnp.bfloat16),
            pltpu.VMEM((rows, live), jnp.float32),
            pltpu.VMEM((row_sets, columns // LANES, LANES), jnp.float32),
            pltpu.VMEM((row_sets, device_total * live, live), jnp.bfloat16),
            pltpu.VMEM((sums, rows, live), jnp.bfloat16),
            pltpu.VMEM((sums, rows, live), jnp.bfloat16),
            pltpu.SemaphoreType.DMA((pieces,)),
            pltpu.SemaphoreType.DMA((5,)),
            pltpu.SemaphoreType.DMA((device_total, pieces)),
            pltpu.SemaphoreType.DMA((hops, pieces)),
            pltpu.SemaphoreType.DMA((device_total, pieces)),
            pltpu.SemaphoreType.DMA((sums, pieces)),
            pltpu.SemaphoreType.DMA((sums, pieces)),
            pltpu.SemaphoreType.DMA((row_sets,)),
            pltpu.SemaphoreType.DMA((row_sets,)),
        ],
        compiler_params=pltpu.CompilerParams(
            collective_id=0, has_side_effects=True, vmem_limit_bytes=48 * 2**20
        ),
        name="merge",
    )(*[pltpu.with_memory_space_constraint(v, pltpu.HBM) for v in operands])


def solution(mesh):
    in_specs = (
        P("rows", ("coarse", "fine")),
        P(("coarse", "fine")),
        P(),
        P(),
        P(),
        P(("coarse", "fine")),
    )
    out_specs = P("rows", ("coarse", "fine"))
    body = functools.partial(per_device, mesh.shape["coarse"], mesh.shape["fine"])
    return jax.shard_map(
        body, mesh=mesh, in_specs=in_specs, out_specs=out_specs, check_vma=False
    )
```
